32 devices in a mesh: section: 2 (over core), et: 2 (over x), dp: 8 (over z, y).
Axes of the slice: x: 2, y: 2, z: 4, core: 2. Of those that a mesh axis runs over, the one named last changes fastest.
Arguments:
- layer_inputs: bfloat16 [2, 1, 2048, 2048], P('section', None, ('dp', 'et')), may hold values from -6 to 6
- out_grad: bfloat16 [1, 2048, 2048], P(None, ('dp', 'et')), may hold values from -6 to 6
- w_gate: bfloat16 [2, 2048, 7168], P('section', None, 'et'), may hold values from -0.125 to 0.125
- w_up: bfloat16 [2, 2048, 7168], P('section', None, 'et'), may hold values from -0.125 to 0.125
- w_down: bfloat16 [2, 2048, 7168], P('section', None, 'et'), may hold values from -0.0625 to 0.0625
- slot_token: int32 [2, 1, 1024], P('section', None, 'dp'), may hold values from -1 to 255, as said below
- slot_gate: float32 [2, 1, 1024], P('section', None, 'dp'), may hold values from 0.1 to 0.9
Outputs:
- in_grad: bfloat16 [2, 1, 2048, 2048], P('section', None, ('dp', 'et'))
- gate_w_grad: bfloat16 [2, 2048, 7168], P('section', 'dp', 'et')
- up_w_grad: bfloat16 [2, 2048, 7168], P('section', 'dp', 'et')
- down_w_grad: bfloat16 [2, 2048, 7168], P('section', 'dp', 'et')
- gate_value_grad: float32 [2, 1, 1024], P('section', None, 'dp')
The draws below stay inside these ranges and needn't reach their ends.
Inputs may be any that keep to these rules, and one draw needn't show every extreme that they name: `slot_token`: each layout (one section, micro-batch and replica) holds distinct tokens of its replica in rising order in its first slots and -1 in the rest; from 64 to 128 slots are live, and in every draw some layout is full.
All inputs are finite; a program needn't handle non-finite values.
Results may differ from the reference program's by a relative error of at most 0.024.
Values may be sent and summed in bfloat16 or wider, within the bound.
No kernel may reach another device: no remote copies, remote signals or barrier semaphores. Data moves between devices by JAX's collectives and lax.ppermute only.
A program may use at most 320 MiB of HBM per device.

```python
import jax
import jax.numpy as jnp
from jax import lax

D = 2048
FF = 7168
MB = 1
TOK = 256
SECTIONS = 2
SLOTS = 128
TOKENS = 2048
ALL_SLOTS = 1024
N_ET = 2
N_DP = 8


def draw_slot_token(key, part):
    layout_count = SECTIONS * MB * (ALL_SLOTS // SLOTS)
    key_list = jax.random.split(key, layout_count + 1)
    full_index = jax.random.randint(key_list[layout_count], (), 0, layout_count)

    def layout(sub_key, position):
        pick_key, live_key = jax.random.split(sub_key)
        chosen = jnp.sort(jax.random.permutation(pick_key, TOK)[:SLOTS])
        live_count = jax.random.randint(live_key, (), SLOTS // 2, SLOTS + 1)
        live_count = jnp.where(position == full_index, SLOTS, live_count)
        slot_place = jnp.arange(SLOTS)
        return jnp.where(slot_place < live_count, chosen, -1).astype(jnp.int32)
    drawn = jax.vmap(layout)(key_list[:layout_count], jnp.arange(layout_count))
    return drawn.reshape(SECTIONS, MB, ALL_SLOTS)


def block_levels(key, shape, cuts, least, high):
    level, own = 1.0, jax.random.fold_in(key, 6)
    for dim, parts in cuts:
        draws = jnp.exp(jax.random.uniform(jax.random.fold_in(own, dim), (parts,), jnp.float32, least / len(cuts), high / len(cuts)))
        level = level * jnp.repeat(draws, shape[dim] // parts).reshape([-1 if axis == dim else 1 for axis in range(len(shape))])
    return level


def centred(own_key, shape, spread, reach, cuts=(), dtype=jnp.bfloat16):
    entries = jax.random.normal(own_key, shape, jnp.float32) * spread
    if len(cuts) > 0:
        entries = block_levels(own_key, shape, cuts, -0.22, 0.18) * entries
    return jnp.clip(entries, min=-reach, max=reach).astype(dtype)


def setup_inputs(seed: int = 0) -> dict:
    arg_keys = jax.random.split(jax.random.key(seed), 8)
    return {
        "layer_inputs": centred(arg_keys[0], (SECTIONS, MB, TOKENS, D), 1.0, 6.0, ((0, 2), (2, 16))),
        "out_grad": centred(arg_keys[1], (MB, TOKENS, D), 1.0, 6.0, ((1, 16),)),
        "w_gate": centred(arg_keys[2], (SECTIONS, D, FF), D ** -0.5, 0.125, ((0, 2), (2, 2))),
        "w_up": centred(arg_keys[3], (SECTIONS, D, FF), D ** -0.5, 0.125, ((0, 2), (2, 2))),
        "w_down": centred(arg_keys[4], (SECTIONS, D, FF), FF ** -0.5, 0.0625, ((0, 2), (2, 2))),
        "slot_token": draw_slot_token(jax.random.fold_in(arg_keys[7], 71), 0),
        "slot_gate": jnp.clip(0.1 + 0.79999997 * jax.random.uniform(arg_keys[6], (SECTIONS, MB, ALL_SLOTS), jnp.float32) ** block_levels(arg_keys[6], (SECTIONS, MB, ALL_SLOTS), ((0, 2), (2, 8)), -0.2, 0.2), 0.1, 0.9),
    }


def rounded(value):
    return lax.optimization_barrier(value.astype(jnp.bfloat16))


def matmul(left, right):
    return jnp.dot(left.astype(jnp.float32), right.astype(jnp.float32), precision=lax.Precision.HIGHEST)


def slice_backward(x_rows, g_rows, gates, w_one, w_three, w_two):
    pre_gate = matmul(x_rows, w_one)
    pre_up = matmul(x_rows, w_three)
    sigma = jax.nn.sigmoid(pre_gate)
    active = pre_gate * sigma
    hidden = rounded(active * pre_up)
    back_hidden = matmul(g_rows, w_two)
    gate_part = jnp.sum(hidden.astype(jnp.float32) * back_hidden, axis=1)
    scaled_back = gates[:, None] * back_hidden
    grad_pre_gate = rounded(scaled_back * pre_up * sigma * (1.0 + pre_gate * (1.0 - sigma)))
    grad_pre_up = rounded(scaled_back * active)
    scaled_rows = rounded(gates[:, None] * g_rows.astype(jnp.float32))
    grad_one = matmul(x_rows.T, grad_pre_gate)
    grad_three = matmul(x_rows.T, grad_pre_up)
    grad_two = matmul(scaled_rows.T, hidden)
    rows_back = rounded(matmul(grad_pre_gate, w_one.T) + matmul(grad_pre_up, w_three.T))
    return rows_back, gate_part, grad_one, grad_three, grad_two


def replica_backward(x_rep, g_rep, slots, gates, w_one, w_three, w_two):
    live_mask = slots >= 0
    safe_slots = jnp.clip(slots, 0, TOK - 1).astype(jnp.int32)
    x_rows = jnp.where(live_mask[:, None], x_rep[safe_slots], jnp.zeros((), jnp.bfloat16)).astype(jnp.bfloat16)
    g_rows = jnp.where(live_mask[:, None], g_rep[safe_slots], jnp.zeros((), jnp.bfloat16)).astype(jnp.bfloat16)
    group_width = FF // N_ET

    def per_slice(group_index):
        start = group_index * group_width
        piece_one = lax.dynamic_slice_in_dim(w_one, start, group_width, 1)
        piece_three = lax.dynamic_slice_in_dim(w_three, start, group_width, 1)
        piece_two = lax.dynamic_slice_in_dim(w_two, start, group_width, 1)
        return slice_backward(x_rows, g_rows, gates, piece_one, piece_three, piece_two)

    rows_back, gate_parts, grad_one, grad_three, grad_two = lax.map(per_slice, jnp.arange(N_ET).astype(jnp.int32))
    rows_total = jnp.sum(rows_back.astype(jnp.float32), axis=0)
    token_back = jnp.zeros((TOK, D), jnp.float32).at[safe_slots].add(
        jnp.where(live_mask[:, None], rows_total, jnp.zeros((), jnp.float32)))
    in_grad_rep = (g_rep.astype(jnp.float32) + token_back).astype(jnp.bfloat16)
    gate_grad = jnp.sum(gate_parts, axis=0)

    def joined(stacked):
        return jnp.moveaxis(stacked, 0, 1).reshape(D, FF)

    return in_grad_rep, gate_grad, (joined(grad_one), joined(grad_three), joined(grad_two))


def reference(layer_inputs, out_grad, w_gate, w_up, w_down, slot_token, slot_gate):
    incoming = out_grad.reshape(MB, N_DP, TOK, D)
    segment_in_grads = [None] * SECTIONS
    segment_gate_grads = [None] * SECTIONS
    segment_weight_grads = [None] * SECTIONS
    for segment_index in range(SECTIONS - 1, -1, -1):
        inputs_here = layer_inputs[segment_index].reshape(MB, N_DP, TOK, D).swapaxes(0, 1)
        grads_here = incoming.swapaxes(0, 1)
        slots_here = slot_token[segment_index].reshape(MB, N_DP, SLOTS).swapaxes(0, 1)
        gates_here = slot_gate[segment_index].reshape(MB, N_DP, SLOTS).swapaxes(0, 1)
        weight_one = w_gate[segment_index]
        weight_three = w_up[segment_index]
        weight_two = w_down[segment_index]

        def per_replica(totals, pieces):
            x_rep, g_rep, slot_rep, gate_rep = pieces
            replica_sum = [jnp.zeros((D, FF), jnp.float32) for _ in range(3)]
            backs = []
            gate_list = []
            for micro_index in range(MB):
                token_grad, gate_grad, grads = replica_backward(
                    x_rep[micro_index], g_rep[micro_index], slot_rep[micro_index],
                    gate_rep[micro_index], weight_one, weight_three, weight_two)
                backs.append(token_grad)
                gate_list.append(gate_grad)
                replica_sum = [total + piece for total, piece in zip(replica_sum, grads)]
            new_totals = tuple(total + rounded(piece).astype(jnp.float32) for total, piece in zip(totals, replica_sum))
            return new_totals, (jnp.stack(backs), jnp.stack(gate_list))

        start_totals = tuple(jnp.zeros((D, FF), jnp.float32) for _ in range(3))
        totals, (backs, gate_stack) = lax.scan(per_replica, start_totals, (inputs_here, grads_here, slots_here, gates_here))
        incoming = backs.swapaxes(0, 1)
        segment_in_grads[segment_index] = incoming.reshape(MB, TOKENS, D)
        segment_gate_grads[segment_index] = gate_stack.swapaxes(0, 1).reshape(MB, ALL_SLOTS)
        segment_weight_grads[segment_index] = tuple((total * (1.0 / N_DP)).astype(jnp.bfloat16) for total in totals)
    in_grad = jnp.stack(segment_in_grads)
    gate_w_grad = jnp.stack([grads[0] for grads in segment_weight_grads])
    up_w_grad = jnp.stack([grads[1] for grads in segment_weight_grads])
    down_w_grad = jnp.stack([grads[2] for grads in segment_weight_grads])
    gate_value_grad = jnp.stack(segment_gate_grads)
    return (in_grad, gate_w_grad, up_w_grad, down_w_grad, gate_value_grad)
```

```python
import jax
import jax.numpy as jnp
from jax import lax
from jax.experimental import pallas as pl
from jax.experimental.pallas import tpu as pltpu
from jax.sharding import PartitionSpec as P

F32 = jnp.float32
BF16 = jnp.bfloat16
BY_ROWS_T = (((1,), (1,)), ((), ()))
BY_ROWS = (((0,), (0,)), ((), ()))


def tile_of(width, most):
    return max(t for t in range(128, most + 1, 128) if width % t == 0)


def params():
    return pltpu.CompilerParams(
        dimension_semantics=("arbitrary",), vmem_limit_bytes=60 << 20
    )


def held(array):
    return pl.BlockSpec(
        array.shape, lambda i: (0,) * array.ndim, pipeline_mode=pl.Buffered(1)
    )


def columns(rows, tile):
    return pl.BlockSpec((rows, tile), lambda i: (0, i))


def forward_parts(pre_gate, pre_up):
    sigma = jax.nn.sigmoid(pre_gate)
    active = pre_gate * sigma
    slope = pre_up * sigma * (1.0 + pre_gate * (1.0 - sigma))
    return active, slope, active * pre_up


def stacked(refs):
    values = [ref[...] for ref in refs]
    return values[0] if len(values) == 1 else jnp.concatenate(values, axis=0)


def forward_rows(blocks, w_one, w_three):
    count, rows, (width, hidden) = len(blocks), sum(b.shape[0] for b in blocks), w_one.shape
    tile = tile_of(hidden, 512)

    def kernel(*refs):
        x_refs, (one, three, slope_ref, active_ref, hidden_ref) = refs[:count], refs[count:]
        x = stacked(x_refs)
        active, slope, product = forward_parts(
            jnp.dot(x, one[...], preferred_element_type=F32),
            jnp.dot(x, three[...], preferred_element_type=F32),
        )
        slope_ref[...] = slope.astype(BF16)
        active_ref[...] = active.astype(BF16)
        hidden_ref[...] = product.astype(BF16)

    return pl.pallas_call(
        kernel,
        grid=(hidden // tile,),
        in_specs=[held(b) for b in blocks] + [columns(width, tile)] * 2,
        out_specs=[columns(rows, tile)] * 3,
        out_shape=[jax.ShapeDtypeStruct((rows, hidden), BF16)] * 3,
        compiler_params=params(),
        cost_estimate=pl.CostEstimate(
            flops=4 * rows * width * hidden,
            bytes_accessed=4 * width * hidden + 6 * rows * hidden,
            transcendentals=rows * hidden,
        ),
        name="forward_rows",
    )(*blocks, w_one, w_three)


def backward_rows(x, g, gates, w_one, w_three, w_two, parts):
    rows, (width, hidden) = g.shape[0], w_one.shape
    tile = tile_of(hidden, 512)
    fresh = parts is None

    def kernel(*refs):
        if fresh:
            x_ref, g_ref, gate_ref, one, three, two, back_ref, part_ref, slope_ref, active_ref, hidden_ref, total = refs
        else:
            g_ref, gate_ref, one, three, two, slope_ref, active_ref, hidden_ref, back_ref, part_ref, total = refs
        step = pl.program_id(0)

        @pl.when(step == 0)
        def _():
            total[...] = jnp.zeros_like(total)
            part_ref[...] = jnp.zeros_like(part_ref)

        back = jnp.dot(g_ref[...], two[...], preferred_element_type=F32)
        if fresh:
            x = x_ref[...]
            active, slope, product = forward_parts(
                jnp.dot(x, one[...], preferred_element_type=F32),
                jnp.dot(x, three[...], preferred_element_type=F32),
            )
            product = product.astype(BF16)
            slope_ref[...] = slope.astype(BF16)
            active_ref[...] = active.astype(BF16)
            hidden_ref[...] = product
        else:
            active, slope, product = active_ref[...], slope_ref[...], hidden_ref[...]
        part_ref[...] += jnp.sum(product.astype(F32) * back, axis=1, keepdims=True)
        scaled = gate_ref[...] * back
        grad_gate = (scaled * slope.astype(F32)).astype(BF16)
        grad_up = (scaled * active.astype(F32)).astype(BF16)
        total[...] += lax.dot_general(
            grad_gate, one[...], BY_ROWS_T, preferred_element_type=F32
        ) + lax.dot_general(grad_up, three[...], BY_ROWS_T, preferred_element_type=F32)

        @pl.when(step == pl.num_programs(0) - 1)
        def _():
            back_ref[...] = total[...].astype(BF16)

    small = [x, g, gates] if fresh else [g, gates]
    whole = pl.BlockSpec((rows, width), lambda i: (0, 0))
    tiles = [columns(rows, tile)] * 3
    made = jax.ShapeDtypeStruct((rows, hidden), BF16)
    return pl.pallas_call(
        kernel,
        grid=(hidden // tile,),
        in_specs=[held(a) for a in small] + [columns(width, tile)] * 3 + ([] if fresh else tiles),
        out_specs=[whole, pl.BlockSpec((rows, 1), lambda i: (0, 0))] + (tiles if fresh else []),
        out_shape=[jax.ShapeDtypeStruct((rows, width), BF16), jax.ShapeDtypeStruct((rows, 1), F32)]
        + ([made] * 3 if fresh else []),
        scratch_shapes=[pltpu.VMEM((rows, width), F32)],
        compiler_params=params(),
        cost_estimate=pl.CostEstimate(
            flops=(10 if fresh else 6) * rows * width * hidden,
            bytes_accessed=6 * width * hidden,
            transcendentals=rows * hidden,
        ),
        name="backward_rows",
    )(*small, w_one, w_three, w_two, *([] if fresh else parts))


def weight_grads(x_blocks, s_blocks, replica, cut, w_two, groups, scale):
    count, size, (width, hidden) = len(s_blocks), s_blocks[0].shape[0], w_two.shape
    rows = count * size
    tile = tile_of(hidden, 512 if rows <= 1024 else 256)
    sizes = [group[0].shape[0] for group in groups]
    aligned = cut % 128 == 0

    def kernel(*refs):
        x_cuts, refs = refs[1 : 1 + count], refs[1 + count :]
        s_cuts, refs = refs[:count], refs[count:]
        s_refs, two, refs = refs[:count], refs[count], refs[count + 1 :]
        given, refs = refs[: 3 * len(sizes)], refs[3 * len(sizes) :]
        out_one, out_three, out_two, x_turned, s_turned, grad_gate, grad_up, product = refs

        @pl.when(pl.program_id(0) == 0)
        def _():
            x_turned[...] = stacked(x_cuts).T
            s_turned[...] = stacked(s_cuts).T

        back = jnp.dot(stacked(s_refs), two[...], preferred_element_type=F32)
        start = 0
        for index, group_rows in enumerate(sizes):
            slope_ref, active_ref, hidden_ref = given[3 * index : 3 * index + 3]
            piece = back[start : start + group_rows, :]
            here = pl.ds(start, group_rows)
            grad_gate[here, :] = (piece * slope_ref[...].astype(F32)).astype(BF16)
            grad_up[here, :] = (piece * active_ref[...].astype(F32)).astype(BF16)
            product[here, :] = hidden_ref[...]
            start += group_rows

        def put(out, left, right):
            out[...] = (jnp.dot(left[...], right[...], preferred_element_type=F32) * scale).astype(BF16)

        put(out_one, x_turned, grad_gate)
        put(out_three, x_turned, grad_up)
        put(out_two, s_turned, product)

    def by_tile(height):
        return pl.BlockSpec((height, tile), lambda i, at: (0, i))

    def kept_whole(shape, column=None):
        return pl.BlockSpec(shape, lambda i, at: (0, 0 if column is None else at[0]), pipeline_mode=pl.Buffered(1))

    if aligned:
        x_cuts, s_cuts = x_blocks, s_blocks
    else:
        x_cuts, s_cuts = (
            [lax.dynamic_slice_in_dim(b, replica * cut, cut, 1) for b in blocks] for blocks in (x_blocks, s_blocks)
        )
    place = replica if aligned else jnp.zeros_like(replica)
    return pl.pallas_call(
        kernel,
        grid_spec=pltpu.PrefetchScalarGridSpec(
            num_scalar_prefetch=1,
            grid=(hidden // tile,),
            in_specs=[kept_whole((size, cut), 0)] * (2 * count)
            + [kept_whole((size, width))] * count
            + [by_tile(width)]
            + [by_tile(group_rows) for group_rows in sizes for _ in range(3)],
            out_specs=[by_tile(cut)] * 3,
            scratch_shapes=[pltpu.VMEM((cut, rows), BF16)] * 2 + [pltpu.VMEM((rows, tile), BF16)] * 3,
        ),
        out_shape=[jax.ShapeDtypeStruct((cut, hidden), BF16)] * 3,
        compiler_params=params(),
        cost_estimate=pl.CostEstimate(
            flops=2 * rows * width * hidden + 6 * rows * cut * hidden,
            bytes_accessed=2 * width * hidden + 6 * rows * hidden + 6 * cut * hidden,
            transcendentals=0,
        ),
        name="weight_grads",
    )(place.reshape(1).astype(jnp.int32), *x_cuts, *s_cuts, *s_blocks, w_two, *[a for group in groups for a in group])


def ring_of(count):
    if count % 2:
        return list(range(count))
    return list(range(0, count, 2)) + list(range(count - 1, 0, -2))


def around(block, sections, count):
    walk = ring_of(count)

    def shift(step):
        return [
            (s * count + walk[i], s * count + walk[(i + step) % count])
            for s in range(sections)
            for i in range(count)
        ]

    axes = ("section", "dp")
    groups, ahead, behind = [[block]], block, block
    for _ in range((count - 1) // 2):
        ahead = lax.ppermute(ahead, axes, shift(1))
        behind = lax.ppermute(behind, axes, shift(-1))
        groups.append([ahead, behind])
    if count % 2 == 0:
        half = block.shape[0] // 2
        groups.append(
            [
                jnp.concatenate(
                    [
                        lax.ppermute(ahead[:half], axes, shift(1)),
                        lax.ppermute(behind[half:], axes, shift(-1)),
                    ],
                    axis=0,
                )
            ]
        )
    return groups


def per_device(layer_inputs, out_grad, w_gate, w_up, w_down, slot_token, slot_gate):
    sections, replicas = lax.axis_size("section"), lax.axis_size("dp")
    last = lax.axis_index("section") == sections - 1
    half, replica = lax.axis_index("et"), lax.axis_index("dp")
    w_one, w_three, w_two = w_gate[0], w_up[0], w_down[0]
    x_mine, dy_mine = layer_inputs[0, 0], out_grad[0]
    slots, gates = slot_token[0, 0], slot_gate[0, 0][:, None]
    shard, width = x_mine.shape
    cut = width // replicas
    last_only = [(2 * (sections - 1) + e, 2 * (sections - 1) + 1 - e) for e in range(2)]
    first_only = [(e, 1 - e) for e in range(2)]

    def swapped(value, pairs):
        return lax.ppermute(value, ("section", "et"), pairs)

    def selector(of):
        return (slots[:, None] == of * shard + jnp.arange(shard, dtype=jnp.int32)[None, :]).astype(BF16)

    pick_mine, pick_theirs = selector(half), selector(1 - half)

    def picked(mine, theirs):
        return (
            jnp.dot(pick_mine, mine, preferred_element_type=F32)
            + jnp.dot(pick_theirs, theirs, preferred_element_type=F32)
        ).astype(BF16)

    def placed_back(pick, dy, back_mine, back_theirs):
        added = lax.dot_general(pick, back_mine, BY_ROWS, preferred_element_type=F32) + lax.dot_general(
            pick, back_theirs, BY_ROWS, preferred_element_type=F32
        )
        return (dy.astype(F32) + added).astype(BF16)

    dy_theirs = swapped(dy_mine, last_only)
    x_theirs = swapped(x_mine, last_only + first_only)
    x_rows = picked(x_mine, x_theirs)
    g_last = picked(dy_mine, dy_theirs)
    x_groups = around(x_rows, sections, replicas)
    x_blocks = [block for group in x_groups for block in group]

    no_back = lambda: (jnp.zeros(x_rows.shape, BF16), jnp.zeros((x_rows.shape[0], 1), F32))
    back_last, part_last, *own = lax.cond(
        last,
        lambda: tuple(backward_rows(x_rows, g_last, gates, w_one, w_three, w_two, None)),
        lambda: (*no_back(), *forward_rows([x_rows], w_one, w_three)),
    )
    other_last = swapped(back_last, last_only)
    kept = [tuple(own), tuple(forward_rows(x_groups[1], w_one, w_three))]
    ig_mine = placed_back(pick_mine, dy_mine, back_last, other_last)
    ig_theirs = placed_back(pick_theirs, dy_theirs, back_last, other_last)
    down = [(1, 0)]
    dy_first_mine = lax.ppermute(ig_mine, "section", down)
    dy_first_theirs = lax.ppermute(ig_theirs, "section", down)
    kept.append(tuple(forward_rows(x_groups[2], w_one, w_three)))
    g_first = picked(dy_first_mine, dy_first_theirs)
    g_rows = jnp.where(last, g_last, g_first)
    s_rows = (gates * g_rows.astype(F32)).astype(BF16)
    s_blocks = [block for group in around(s_rows, sections, replicas) for block in group]

    back_first, part_first = lax.cond(
        last,
        no_back,
        lambda: tuple(backward_rows(None, g_first, gates, w_one, w_three, w_two, own)),
    )
    other_first = swapped(back_first, first_only)
    ig_first = placed_back(pick_mine, dy_first_mine, back_first, other_first)
    in_grad = jnp.where(last, ig_mine, ig_first)
    part = jnp.where(last, part_last, part_first)[:, 0]
    gate_grad = part + lax.ppermute(part, "et", first_only)
    rest = [block for group in x_groups[3:] for block in group]
    for start in range(0, len(rest), 4):
        kept.append(tuple(forward_rows(rest[start : start + 4], w_one, w_three)))

    grads = weight_grads(x_blocks, s_blocks, replica, cut, w_two, kept, 1.0 / replicas)
    return (in_grad[None, None], *[grad[None] for grad in grads], gate_grad[None, None])


def solution(mesh):
    placed = (
        P("section", None, ("dp", "et"), None),
        P(None, ("dp", "et"), None),
        P("section", None, "et"),
        P("section", None, "et"),
        P("section", None, "et"),
        P("section", None, "dp"),
        P("section", None, "dp"),
    )
    return jax.shard_map(
        per_device,
        mesh=mesh,
        in_specs=placed,
        out_specs=(
            P("section", None, ("dp", "et"), None),
            P("section", "dp", "et"),
            P("section", "dp", "et"),
            P("section", "dp", "et"),
            P("section", None, "dp"),
        ),
        check_vma=False,
    )
```

```python
import jax
import jax.numpy as jnp
from jax import lax
from jax.experimental import pallas as pl
from jax.experimental.pallas import tpu as pltpu
from jax.sharding import PartitionSpec as P

F32 = jnp.float32
BF16 = jnp.bfloat16
BY_ROWS_T = (((1,), (1,)), ((), ()))
BY_ROWS = (((0,), (0,)), ((), ()))


def tile_of(width, most):
    return max(t for t in range(128, most + 1, 128) if width % t == 0)


def params(mib):
    return pltpu.CompilerParams(dimension_semantics=("arbitrary",), vmem_limit_bytes=mib << 20)


def in_hbm(arrays):
    return [pltpu.with_memory_space_constraint(a, pltpu.HBM) for a in arrays]


RESIDENT = pl.BlockSpec(memory_space=pltpu.VMEM)


def load(*arrays):
    count = len(arrays)

    def kernel(*refs):
        copies = [
            pltpu.make_async_copy(refs[i], refs[count + i], refs[2 * count].at[i]) for i in range(count)
        ]
        for copy in copies:
            copy.start()
        for copy in copies:
            copy.wait()

    return pl.pallas_call(
        kernel,
        in_specs=[pl.BlockSpec(memory_space=pltpu.HBM)] * count,
        out_specs=[RESIDENT] * count,
        out_shape=[pltpu.VMEM(a.shape, a.dtype) for a in arrays],
        scratch_shapes=[pltpu.SemaphoreType.DMA((count,))],
        compiler_params=pltpu.CompilerParams(vmem_limit_bytes=1 << 20),
        cost_estimate=pl.CostEstimate(
            flops=0, bytes_accessed=sum(2 * a.size for a in arrays), transcendentals=0
        ),
        name="load",
    )(*in_hbm(arrays))


def slab(tile):
    return pl.ds(pl.multiple_of(pl.program_id(0) * tile, tile), tile)


def held(array):
    return pl.BlockSpec(
        array.shape, lambda i: (0,) * array.ndim, pipeline_mode=pl.Buffered(1)
    )


def columns(rows, tile):
    return pl.BlockSpec((rows, tile), lambda i: (0, i))


def forward_parts(pre_gate, pre_up):
    sigma = jax.nn.sigmoid(pre_gate)
    active = pre_gate * sigma
    slope = pre_up * sigma * (1.0 + pre_gate * (1.0 - sigma))
    return active, slope, active * pre_up


def stacked(refs):
    values = [ref[...] for ref in refs]
    return values[0] if len(values) == 1 else jnp.concatenate(values, axis=0)


def forward_rows(blocks, w_one, w_three):
    count, rows, (width, hidden) = len(blocks), sum(b.shape[0] for b in blocks), w_one.shape
    tile = tile_of(hidden, 512)

    def kernel(*refs):
        x_refs, (one, three, slope_ref, active_ref, hidden_ref) = refs[:count], refs[count:]
        x, here = stacked(x_refs), slab(tile)
        active, slope, product = forward_parts(
            jnp.dot(x, one[:, here], preferred_element_type=F32),
            jnp.dot(x, three[:, here], preferred_element_type=F32),
        )
        slope_ref[...] = slope.astype(BF16)
        active_ref[...] = active.astype(BF16)
        hidden_ref[...] = product.astype(BF16)

    return pl.pallas_call(
        kernel,
        grid=(hidden // tile,),
        in_specs=[held(b) for b in blocks] + [RESIDENT] * 2,
        out_specs=[columns(rows, tile)] * 3,
        out_shape=[pltpu.HBM((rows, hidden), BF16)] * 3,
        compiler_params=params(20),
        cost_estimate=pl.CostEstimate(
            flops=4 * rows * width * hidden,
            bytes_accessed=6 * rows * hidden,
            transcendentals=rows * hidden,
        ),
        name="forward_rows",
    )(*in_hbm(blocks), w_one, w_three)


def backward_rows(active_here, x_blocks, g, gates, w_one, w_three, w_two, parts):
    rows, (width, hidden) = g.shape[0], w_one.shape
    tile = tile_of(hidden, 512)
    count, height = len(x_blocks), sum(b.shape[0] for b in x_blocks)
    parts = parts or []

    def kernel(flag, *refs):
        x_refs, refs = refs[:count], refs[count:]
        g_ref, gate_ref, one, three, two, *refs = refs
        stored, refs = refs[: len(parts)], refs[len(parts) :]
        back_ref, part_ref, slope_ref, active_ref, hidden_ref, total = refs
        step, here = pl.program_id(0), slab(tile)

        @pl.when(step == 0)
        def _():
            total[...] = jnp.zeros_like(total)
            part_ref[...] = jnp.zeros_like(part_ref)

        x = stacked(x_refs)
        active, slope, product = forward_parts(
            jnp.dot(x, one[:, here], preferred_element_type=F32),
            jnp.dot(x, three[:, here], preferred_element_type=F32),
        )
        slope_ref[...] = slope.astype(BF16)
        active_ref[...] = active.astype(BF16)
        hidden_ref[...] = product.astype(BF16)

        @pl.when(flag[0] > 0)
        def _():
            slope_of, active_of, hidden_of = stored if parts else (slope_ref, active_ref, hidden_ref)
            back = jnp.dot(g_ref[...], two[...], preferred_element_type=F32)
            part_ref[...] += jnp.sum(hidden_of[...].astype(F32) * back, axis=1, keepdims=True)
            scaled = gate_ref[...] * back
            grad_gate = (scaled * slope_of[...].astype(F32)).astype(BF16)
            grad_up = (scaled * active_of[...].astype(F32)).astype(BF16)
            total[...] += lax.dot_general(
                grad_gate, one[:, here], BY_ROWS_T, preferred_element_type=F32
            ) + lax.dot_general(grad_up, three[:, here], BY_ROWS_T, preferred_element_type=F32)

        @pl.when(step == pl.num_programs(0) - 1)
        def _():
            back_ref[...] = total[...].astype(BF16)

    return pl.pallas_call(
        kernel,
        grid=(hidden // tile,),
        in_specs=[pl.BlockSpec(memory_space=pltpu.SMEM)]
        + [held(a) for a in (*x_blocks, g, gates)]
        + [RESIDENT] * 2
        + [columns(width, tile)]
        + [columns(rows, tile)] * len(parts),
        out_specs=[pl.BlockSpec((rows, width), lambda i: (0, 0)), pl.BlockSpec((rows, 1), lambda i: (0, 0))]
        + [columns(height, tile)] * 3,
        out_shape=[jax.ShapeDtypeStruct((rows, width), BF16), jax.ShapeDtypeStruct((rows, 1), F32)]
        + [pltpu.HBM((height, hidden), BF16)] * 3,
        scratch_shapes=[pltpu.VMEM((rows, width), F32)],
        compiler_params=params(20),
        cost_estimate=pl.CostEstimate(
            flops=(6 * rows + 4 * height) * width * hidden,
            bytes_accessed=2 * width * hidden,
            transcendentals=height * hidden,
        ),
        name="backward_rows",
    )(active_here.astype(jnp.int32).reshape(1), *in_hbm(x_blocks), g, gates, w_one, w_three, w_two, *in_hbm(parts))


def weight_grads(x_blocks, s_blocks, replica, cut, w_two, groups, before, scale):
    count, size, (width, hidden) = len(s_blocks), s_blocks[0].shape[0], w_two.shape
    rows = count * size
    tile = tile_of(hidden, 512 if rows <= 1024 else 256)
    sizes = [group[0].shape[0] for group in groups]
    aligned = cut % 128 == 0

    def kernel(*refs):
        x_cuts, refs = refs[1 : 1 + count], refs[1 + count :]
        s_cuts, refs = refs[:count], refs[count:]
        s_refs, two, refs = refs[:count], refs[count], refs[count + 1 :]
        given, refs = refs[: 3 * len(sizes)], refs[3 * len(sizes) :]
        sums, refs = refs[: len(before)], refs[len(before) :]
        out_one, out_three, out_two, x_turned, s_turned, grad_gate, grad_up, product = refs

        @pl.when(pl.program_id(0) == 0)
        def _():
            x_turned[...] = stacked(x_cuts).T
            s_turned[...] = stacked(s_cuts).T

        back = jnp.dot(stacked(s_refs), two[...], preferred_element_type=F32)
        start = 0
        for index, group_rows in enumerate(sizes):
            slope_ref, active_ref, hidden_ref = given[3 * index : 3 * index + 3]
            piece = back[start : start + group_rows, :]
            here = pl.ds(start, group_rows)
            grad_gate[here, :] = (piece * slope_ref[...].astype(F32)).astype(BF16)
            grad_up[here, :] = (piece * active_ref[...].astype(F32)).astype(BF16)
            product[here, :] = hidden_ref[...]
            start += group_rows

        for index, (out, left, right) in enumerate(
            ((out_one, x_turned, grad_gate), (out_three, x_turned, grad_up), (out_two, s_turned, product))
        ):
            value = jnp.dot(left[...], right[...], preferred_element_type=F32)
            if sums:
                value = sums[index][...] + value
            out[...] = value if scale is None else (value * scale).astype(BF16)

    def by_tile(height):
        return pl.BlockSpec((height, tile), lambda i, at: (0, i))

    def kept_whole(shape, column=None):
        return pl.BlockSpec(shape, lambda i, at: (0, 0 if column is None else at[0]), pipeline_mode=pl.Buffered(1))

    if aligned:
        x_cuts, s_cuts = x_blocks, s_blocks
    else:
        x_cuts, s_cuts = (
            [lax.dynamic_slice_in_dim(b, replica * cut, cut, 1) for b in blocks] for blocks in (x_blocks, s_blocks)
        )
    place = replica if aligned else jnp.zeros_like(replica)
    return pl.pallas_call(
        kernel,
        grid_spec=pltpu.PrefetchScalarGridSpec(
            num_scalar_prefetch=1,
            grid=(hidden // tile,),
            in_specs=[kept_whole((size, cut), 0)] * (2 * count)
            + [kept_whole((size, width))] * count
            + [by_tile(width)]
            + [by_tile(group_rows) for group_rows in sizes for _ in range(3)]
            + [by_tile(cut)] * len(before),
            out_specs=[by_tile(cut)] * 3,
            scratch_shapes=[pltpu.VMEM((cut, rows), BF16)] * 2 + [pltpu.VMEM((rows, tile), BF16)] * 3,
        ),
        out_shape=[pltpu.HBM((cut, hidden), F32 if scale is None else BF16)] * 3,
        compiler_params=params(40),
        cost_estimate=pl.CostEstimate(
            flops=2 * rows * width * hidden + 6 * rows * cut * hidden,
            bytes_accessed=2 * width * hidden + 6 * rows * hidden + 6 * cut * hidden,
            transcendentals=0,
        ),
        name="weight_grads",
    )(place.reshape(1).astype(jnp.int32), *in_hbm([*x_cuts, *s_cuts, *s_blocks, w_two, *[a for group in groups for a in group], *before]))


def ring_of(count):
    if count % 2:
        return list(range(count))
    return list(range(0, count, 2)) + list(range(count - 1, 0, -2))


def around(block, sections, count):
    walk = ring_of(count)

    def shift(step):
        return [
            (s * count + walk[i], s * count + walk[(i + step) % count])
            for s in range(sections)
            for i in range(count)
        ]

    axes = ("section", "dp")
    groups, ahead, behind = [[block]], block, block
    for _ in range(1, (count + 1) // 2):
        ahead = lax.ppermute(ahead, axes, shift(1))
        behind = lax.ppermute(behind, axes, shift(-1))
        groups.append([ahead, behind])
    if count % 2 == 0:
        half = block.shape[0] // 2
        front = lax.ppermute(ahead[:half], axes, shift(1))
        rear = lax.ppermute(behind[half:], axes, shift(-1))
        groups.append([jnp.concatenate([front, rear], axis=0)])
    return groups


def per_device(layer_inputs, out_grad, w_gate, w_up, w_down, slot_token, slot_gate):
    sections, replicas = lax.axis_size("section"), lax.axis_size("dp")
    last = lax.axis_index("section") == sections - 1
    half, replica = lax.axis_index("et"), lax.axis_index("dp")
    w_one, w_three, w_two = w_gate[0], w_up[0], w_down[0]
    x_mine, dy_mine = layer_inputs[0, 0], out_grad[0]
    slots, gates = slot_token[0, 0], slot_gate[0, 0][:, None]
    shard, width = x_mine.shape
    cut = width // replicas
    last_only = [(2 * (sections - 1) + e, 2 * (sections - 1) + 1 - e) for e in range(2)]
    first_only = [(e, 1 - e) for e in range(2)]

    def swapped(value, pairs):
        return lax.ppermute(value, ("section", "et"), pairs)

    def selector(of):
        return (slots[:, None] == of * shard + jnp.arange(shard, dtype=jnp.int32)[None, :]).astype(BF16)

    pick_mine, pick_theirs = selector(half), selector(1 - half)

    def picked(mine, theirs):
        return (
            jnp.dot(pick_mine, mine, preferred_element_type=F32)
            + jnp.dot(pick_theirs, theirs, preferred_element_type=F32)
        ).astype(BF16)

    def placed_back(pick, dy, back_mine, back_theirs):
        added = lax.dot_general(pick, back_mine, BY_ROWS, preferred_element_type=F32) + lax.dot_general(
            pick, back_theirs, BY_ROWS, preferred_element_type=F32
        )
        return (dy.astype(F32) + added).astype(BF16)

    dy_theirs = swapped(dy_mine, last_only)
    x_theirs = swapped(x_mine, last_only + first_only)
    w_one, w_three = load(w_one, w_three)
    x_rows = picked(x_mine, x_theirs)
    g_last = picked(dy_mine, dy_theirs)
    x_groups = around(x_rows, sections, replicas)

    def joined(groups):
        return [block for group in groups for block in group]

    back_last, part_last, *own = backward_rows(last, [x_rows], g_last, gates, w_one, w_three, w_two, None)
    other_last = swapped(back_last, last_only)
    ig_mine = placed_back(pick_mine, dy_mine, back_last, other_last)
    ig_theirs = placed_back(pick_theirs, dy_theirs, back_last, other_last)
    dy_first_mine = lax.ppermute(ig_mine, "section", [(1, 0)])
    dy_first_theirs = lax.ppermute(ig_theirs, "section", [(1, 0)])
    kept = [tuple(own), tuple(forward_rows(x_groups[1], w_one, w_three))]
    g_first = picked(dy_first_mine, dy_first_theirs)
    g_rows = jnp.where(last, g_last, g_first)
    s_rows = (gates * g_rows.astype(F32)).astype(BF16)
    s_groups = around(s_rows, sections, replicas)

    back_first, part_first, *third = backward_rows(
        jnp.logical_not(last), x_groups[2], g_first, gates, w_one, w_three, w_two, own
    )
    kept.append(tuple(third))
    other_first = swapped(back_first, first_only)
    part = jnp.where(last, part_last, part_first)[:, 0]
    gate_grad = part + lax.ppermute(part, "et", first_only)
    ig_first = placed_back(pick_mine, dy_first_mine, back_first, other_first)
    in_grad = jnp.where(last, ig_mine, ig_first)
    rest = joined(x_groups[3:])
    late = []
    for start in range(0, len(rest), 4):
        late.append(tuple(forward_rows(rest[start : start + 4], w_one, w_three)))

    sums = weight_grads(joined(x_groups[:3]), joined(s_groups[:3]), replica, cut, w_two, kept, [], None)
    far = joined(s_groups[3:])
    for index, group in enumerate(late):
        scale = 1.0 / replicas if index == len(late) - 1 else None
        here = slice(4 * index, 4 * index + 4)
        sums = weight_grads(rest[here], far[here], replica, cut, w_two, [group], sums, scale)
    return (in_grad[None, None], *[grad[None] for grad in sums], gate_grad[None, None])


def solution(mesh):
    placed = (
        P("section", None, ("dp", "et"), None),
        P(None, ("dp", "et"), None),
        P("section", None, "et"),
        P("section", None, "et"),
        P("section", None, "et"),
        P("section", None, "dp"),
        P("section", None, "dp"),
    )

    return jax.shard_map(
        per_device,
        mesh=mesh,
        in_specs=placed,
        out_specs=(
            P("section", None, ("dp", "et"), None),
            P("section", "dp", "et"),
            P("section", "dp", "et"),
            P("section", "dp", "et"),
            P("section", None, "dp"),
        ),
        check_vma=False,
    )
```

```python
import jax
import jax.numpy as jnp
from jax import lax
from jax.experimental import pallas as pl
from jax.experimental.pallas import tpu as pltpu
from jax.sharding import PartitionSpec as P

F32 = jnp.float32
BF16 = jnp.bfloat16
BY_ROWS_T = (((1,), (1,)), ((), ()))
BY_ROWS = (((0,), (0,)), ((), ()))


def tile_of(width, most):
    return max(t for t in range(128, most + 1, 128) if width % t == 0)


def params(mib):
    return pltpu.CompilerParams(dimension_semantics=("arbitrary",), vmem_limit_bytes=mib << 20)


def in_hbm(arrays):
    return [pltpu.with_memory_space_constraint(a, pltpu.HBM) for a in arrays]


RESIDENT = pl.BlockSpec(memory_space=pltpu.VMEM)


def load(*arrays):
    count = len(arrays)

    def kernel(*refs):
        copies = [
            pltpu.make_async_copy(refs[i], refs[count + i], refs[2 * count].at[i]) for i in range(count)
        ]
        for copy in copies:
            copy.start()
        for copy in copies:
            copy.wait()

    return pl.pallas_call(
        kernel,
        in_specs=[pl.BlockSpec(memory_space=pltpu.HBM)] * count,
        out_specs=[RESIDENT] * count,
        out_shape=[pltpu.VMEM(a.shape, a.dtype) for a in arrays],
        scratch_shapes=[pltpu.SemaphoreType.DMA((count,))],
        compiler_params=pltpu.CompilerParams(vmem_limit_bytes=1 << 20),
        cost_estimate=pl.CostEstimate(
            flops=0, bytes_accessed=sum(2 * a.size for a in arrays), transcendentals=0
        ),
        name="load",
    )(*in_hbm(arrays))


def slab(tile):
    return pl.ds(pl.multiple_of(pl.program_id(0) * tile, tile), tile)


def held(array):
    return pl.BlockSpec(
        array.shape, lambda i: (0,) * array.ndim, pipeline_mode=pl.Buffered(1)
    )


def columns(rows, tile):
    return pl.BlockSpec((rows, tile), lambda i: (0, i))


def forward_parts(pre_gate, pre_up):
    sigma = jax.nn.sigmoid(pre_gate)
    active = pre_gate * sigma
    slope = pre_up * sigma * (1.0 + pre_gate * (1.0 - sigma))
    return active, slope, active * pre_up


def stacked(refs):
    values = [ref[...] for ref in refs]
    return values[0] if len(values) == 1 else jnp.concatenate(values, axis=0)


def forward_rows(blocks, w_one, w_three):
    count, rows, (width, hidden) = len(blocks), sum(b.shape[0] for b in blocks), w_one.shape
    tile = tile_of(hidden, 512)

    def kernel(*refs):
        x_refs, (one, three, slope_ref, active_ref, hidden_ref) = refs[:count], refs[count:]
        x, here = stacked(x_refs), slab(tile)
        active, slope, product = forward_parts(
            jnp.dot(x, one[:, here], preferred_element_type=F32),
            jnp.dot(x, three[:, here], preferred_element_type=F32),
        )
        slope_ref[...] = slope.astype(BF16)
        active_ref[...] = active.astype(BF16)
        hidden_ref[...] = product.astype(BF16)

    return pl.pallas_call(
        kernel,
        grid=(hidden // tile,),
        in_specs=[held(b) for b in blocks] + [RESIDENT] * 2,
        out_specs=[columns(rows, tile)] * 3,
        out_shape=[pltpu.HBM((rows, hidden), BF16)] * 3,
        compiler_params=params(20),
        cost_estimate=pl.CostEstimate(
            flops=4 * rows * width * hidden,
            bytes_accessed=6 * rows * hidden,
            transcendentals=rows * hidden,
        ),
        name="forward_rows",
    )(*in_hbm(blocks), w_one, w_three)


def backward_rows(active_here, x_blocks, g, gates, w_one, w_three, w_two, parts):
    rows, (width, hidden) = g.shape[0], w_one.shape
    tile = tile_of(hidden, 512)
    count, height = len(x_blocks), sum(b.shape[0] for b in x_blocks)
    parts = parts or []

    def kernel(flag, *refs):
        x_refs, refs = refs[:count], refs[count:]
        g_ref, gate_ref, one, three, two, *refs = refs
        stored, refs = refs[: len(parts)], refs[len(parts) :]
        back_ref, part_ref, slope_ref, active_ref, hidden_ref, total = refs
        step, here = pl.program_id(0), slab(tile)

        @pl.when(step == 0)
        def _():
            total[...] = jnp.zeros_like(total)
            part_ref[...] = jnp.zeros_like(part_ref)

        x = stacked(x_refs)
        active, slope, product = forward_parts(
            jnp.dot(x, one[:, here], preferred_element_type=F32),
            jnp.dot(x, three[:, here], preferred_element_type=F32),
        )
        slope_ref[...] = slope.astype(BF16)
        active_ref[...] = active.astype(BF16)
        hidden_ref[...] = product.astype(BF16)

        @pl.when(flag[0] > 0)
        def _():
            slope_of, active_of, hidden_of = stored if parts else (slope_ref, active_ref, hidden_ref)
            back = jnp.dot(g_ref[...], two[...], preferred_element_type=F32)
            part_ref[...] += jnp.sum(hidden_of[...].astype(F32) * back, axis=1, keepdims=True)
            scaled = gate_ref[...] * back
            grad_gate = (scaled * slope_of[...].astype(F32)).astype(BF16)
            grad_up = (scaled * active_of[...].astype(F32)).astype(BF16)
            total[...] += lax.dot_general(
                grad_gate, one[:, here], BY_ROWS_T, preferred_element_type=F32
            ) + lax.dot_general(grad_up, three[:, here], BY_ROWS_T, preferred_element_type=F32)

        @pl.when(step == pl.num_programs(0) - 1)
        def _():
            back_ref[...] = total[...].astype(BF16)

    return pl.pallas_call(
        kernel,
        grid=(hidden // tile,),
        in_specs=[pl.BlockSpec(memory_space=pltpu.SMEM)]
        + [held(a) for a in (*x_blocks, g, gates)]
        + [RESIDENT] * 2
        + [columns(width, tile)]
        + [columns(rows, tile)] * len(parts),
        out_specs=[pl.BlockSpec((rows, width), lambda i: (0, 0)), pl.BlockSpec((rows, 1), lambda i: (0, 0))]
        + [columns(height, tile)] * 3,
        out_shape=[jax.ShapeDtypeStruct((rows, width), BF16), jax.ShapeDtypeStruct((rows, 1), F32)]
        + [pltpu.HBM((height, hidden), BF16)] * 3,
        scratch_shapes=[pltpu.VMEM((rows, width), F32)],
        compiler_params=params(20),
        cost_estimate=pl.CostEstimate(
            flops=(6 * rows + 4 * height) * width * hidden,
            bytes_accessed=2 * width * hidden,
            transcendentals=height * hidden,
        ),
        name="backward_rows",
    )(active_here.astype(jnp.int32).reshape(1), *in_hbm(x_blocks), g, gates, w_one, w_three, w_two, *in_hbm(parts))


def weight_grads(x_blocks, s_blocks, replica, cut, w_two, groups, before, scale):
    count, size, (width, hidden) = len(s_blocks), s_blocks[0].shape[0], w_two.shape
    rows = count * size
    tile = tile_of(hidden, 512 if rows <= 1024 else 256)
    sizes = [group[0].shape[0] for group in groups]
    aligned = cut % 128 == 0

    def kernel(*refs):
        x_cuts, refs = refs[1 : 1 + count], refs[1 + count :]
        s_cuts, refs = refs[:count], refs[count:]
        s_refs, two, refs = refs[:count], refs[count], refs[count + 1 :]
        given, refs = refs[: 3 * len(sizes)], refs[3 * len(sizes) :]
        sums, refs = refs[: len(before)], refs[len(before) :]
        out_one, out_three, out_two, x_turned, s_turned, grad_gate, grad_up, product = refs

        @pl.when(pl.program_id(0) == 0)
        def _():
            x_turned[...] = stacked(x_cuts).T
            s_turned[...] = stacked(s_cuts).T

        here_all = slab(tile)
        back = jnp.dot(stacked(s_refs), two[...], preferred_element_type=F32)
        start = 0
        for index, group_rows in enumerate(sizes):
            slope_ref, active_ref, hidden_ref = given[3 * index : 3 * index + 3]
            piece = back[start : start + group_rows, :]
            here = pl.ds(start, group_rows)
            grad_gate[here, :] = (piece * slope_ref[...].astype(F32)).astype(BF16)
            grad_up[here, :] = (piece * active_ref[...].astype(F32)).astype(BF16)
            product[here, :] = hidden_ref[...]
            start += group_rows

        for index, (out, left, right) in enumerate(
            ((out_one, x_turned, grad_gate), (out_three, x_turned, grad_up), (out_two, s_turned, product))
        ):
            value = jnp.dot(left[...], right[...], preferred_element_type=F32)
            if sums:
                value = sums[index][:, here_all] + value
            if scale is None:
                out[:, here_all] = value
            else:
                out[...] = (value * scale).astype(BF16)

    def by_tile(height):
        return pl.BlockSpec((height, tile), lambda i, at: (0, i))

    def kept_whole(shape, column=None):
        return pl.BlockSpec(shape, lambda i, at: (0, 0 if column is None else at[0]), pipeline_mode=pl.Buffered(1))

    if aligned:
        x_cuts, s_cuts = x_blocks, s_blocks
    else:
        x_cuts, s_cuts = (
            [lax.dynamic_slice_in_dim(b, replica * cut, cut, 1) for b in blocks] for blocks in (x_blocks, s_blocks)
        )
    place = replica if aligned else jnp.zeros_like(replica)
    return pl.pallas_call(
        kernel,
        grid_spec=pltpu.PrefetchScalarGridSpec(
            num_scalar_prefetch=1,
            grid=(hidden // tile,),
            in_specs=[kept_whole((size, cut), 0)] * (2 * count)
            + [kept_whole((size, width))] * count
            + [by_tile(width)]
            + [by_tile(group_rows) for group_rows in sizes for _ in range(3)]
            + [RESIDENT] * len(before),
            out_specs=[RESIDENT if scale is None else by_tile(cut)] * 3,
            scratch_shapes=[pltpu.VMEM((cut, rows), BF16)] * 2 + [pltpu.VMEM((rows, tile), BF16)] * 3,
        ),
        out_shape=[pltpu.VMEM((cut, hidden), F32) if scale is None else pltpu.HBM((cut, hidden), BF16)] * 3,
        compiler_params=params(24),
        cost_estimate=pl.CostEstimate(
            flops=2 * rows * width * hidden + 6 * rows * cut * hidden,
            bytes_accessed=2 * width * hidden + 6 * rows * hidden + 6 * cut * hidden,
            transcendentals=0,
        ),
        name="weight_grads",
    )(place.reshape(1).astype(jnp.int32), *in_hbm([*x_cuts, *s_cuts, *s_blocks, w_two]), *in_hbm([a for group in groups for a in group]), *before)


def ring_of(count):
    if count % 2:
        return list(range(count))
    return list(range(0, count, 2)) + list(range(count - 1, 0, -2))


def around(block, sections, count):
    walk = ring_of(count)

    def shift(step):
        return [
            (s * count + walk[i], s * count + walk[(i + step) % count])
            for s in range(sections)
            for i in range(count)
        ]

    axes = ("section", "dp")
    groups, ahead, behind = [[block]], block, block
    for _ in range(1, (count + 1) // 2):
        ahead = lax.ppermute(ahead, axes, shift(1))
        behind = lax.ppermute(behind, axes, shift(-1))
        groups.append([ahead, behind])
    if count % 2 == 0:
        half = block.shape[0] // 2
        front = lax.ppermute(ahead[:half], axes, shift(1))
        rear = lax.ppermute(behind[half:], axes, shift(-1))
        groups.append([jnp.concatenate([front, rear], axis=0)])
    return groups


def per_device(layer_inputs, out_grad, w_gate, w_up, w_down, slot_token, slot_gate):
    sections, replicas = lax.axis_size("section"), lax.axis_size("dp")
    last = lax.axis_index("section") == sections - 1
    half, replica = lax.axis_index("et"), lax.axis_index("dp")
    w_one, w_three, w_two = w_gate[0], w_up[0], w_down[0]
    x_mine, dy_mine = layer_inputs[0, 0], out_grad[0]
    slots, gates = slot_token[0, 0], slot_gate[0, 0][:, None]
    shard, width = x_mine.shape
    cut = width // replicas
    last_only = [(2 * (sections - 1) + e, 2 * (sections - 1) + 1 - e) for e in range(2)]
    first_only = [(e, 1 - e) for e in range(2)]

    def swapped(value, pairs):
        return lax.ppermute(value, ("section", "et"), pairs)

    def selector(of):
        return (slots[:, None] == of * shard + jnp.arange(shard, dtype=jnp.int32)[None, :]).astype(BF16)

    pick_mine, pick_theirs = selector(half), selector(1 - half)

    def picked(mine, theirs):
        return (
            jnp.dot(pick_mine, mine, preferred_element_type=F32)
            + jnp.dot(pick_theirs, theirs, preferred_element_type=F32)
        ).astype(BF16)

    def placed_back(pick, dy, back_mine, back_theirs):
        added = lax.dot_general(pick, back_mine, BY_ROWS, preferred_element_type=F32) + lax.dot_general(
            pick, back_theirs, BY_ROWS, preferred_element_type=F32
        )
        return (dy.astype(F32) + added).astype(BF16)

    dy_theirs = swapped(dy_mine, last_only)
    x_theirs = swapped(x_mine, last_only + first_only)
    w_one, w_three = load(w_one, w_three)
    x_rows = picked(x_mine, x_theirs)
    g_last = picked(dy_mine, dy_theirs)
    x_groups = around(x_rows, sections, replicas)

    def joined(groups):
        return [block for group in groups for block in group]

    back_last, part_last, *own = backward_rows(last, [x_rows], g_last, gates, w_one, w_three, w_two, None)
    other_last = swapped(back_last, last_only)
    ig_mine = placed_back(pick_mine, dy_mine, back_last, other_last)
    ig_theirs = placed_back(pick_theirs, dy_theirs, back_last, other_last)
    dy_first_mine = lax.ppermute(ig_mine, "section", [(1, 0)])
    dy_first_theirs = lax.ppermute(ig_theirs, "section", [(1, 0)])
    kept = [tuple(own), tuple(forward_rows(x_groups[1], w_one, w_three))]
    g_first = picked(dy_first_mine, dy_first_theirs)
    g_rows = jnp.where(last, g_last, g_first)
    s_rows = (gates * g_rows.astype(F32)).astype(BF16)
    s_groups = around(s_rows, sections, replicas)

    back_first, part_first, *third = backward_rows(
        jnp.logical_not(last), x_groups[2], g_first, gates, w_one, w_three, w_two, own
    )
    kept.append(tuple(third))
    other_first = swapped(back_first, first_only)
    part = jnp.where(last, part_last, part_first)[:, 0]
    gate_grad = part + lax.ppermute(part, "et", first_only)
    ig_first = placed_back(pick_mine, dy_first_mine, back_first, other_first)
    in_grad = jnp.where(last, ig_mine, ig_first)
    rest = joined(x_groups[3:])
    late = []
    for start in range(0, len(rest), 4):
        late.append(tuple(forward_rows(rest[start : start + 4], w_one, w_three)))

    sums = weight_grads(joined(x_groups[:3]), joined(s_groups[:3]), replica, cut, w_two, kept, [], None)
    far = joined(s_groups[3:])
    for index, group in enumerate(late):
        scale = 1.0 / replicas if index == len(late) - 1 else None
        here = slice(4 * index, 4 * index + 4)
        sums = weight_grads(rest[here], far[here], replica, cut, w_two, [group], sums, scale)
    return (in_grad[None, None], *[grad[None] for grad in sums], gate_grad[None, None])


def solution(mesh):
    placed = (
        P("section", None, ("dp", "et"), None),
        P(None, ("dp", "et"), None),
        P("section", None, "et"),
        P("section", None, "et"),
        P("section", None, "et"),
        P("section", None, "dp"),
        P("section", None, "dp"),
    )

    return jax.shard_map(
        per_device,
        mesh=mesh,
        in_specs=placed,
        out_specs=(
            P("section", None, ("dp", "et"), None),
            P("section", "dp", "et"),
            P("section", "dp", "et"),
            P("section", "dp", "et"),
            P("section", None, "dp"),
        ),
        check_vma=False,
    )
```

```python
import jax
import jax.numpy as jnp
from jax import lax
from jax.experimental import pallas as pl
from jax.experimental.pallas import tpu as pltpu
from jax.sharding import PartitionSpec as P

F32 = jnp.float32
BF16 = jnp.bfloat16
BY_ROWS_T = (((1,), (1,)), ((), ()))
BY_ROWS = (((0,), (0,)), ((), ()))


def tile_of(width, most):
    return max(t for t in range(128, most + 1, 128) if width % t == 0)


def params(mib):
    return pltpu.CompilerParams(dimension_semantics=("arbitrary",), vmem_limit_bytes=mib << 20)


def in_hbm(arrays):
    return [pltpu.with_memory_space_constraint(a, pltpu.HBM) for a in arrays]


RESIDENT = pl.BlockSpec(memory_space=pltpu.VMEM)


def load(*arrays):
    count = len(arrays)

    def kernel(*refs):
        copies = [
            pltpu.make_async_copy(refs[i], refs[count + i], refs[2 * count].at[i]) for i in range(count)
        ]
        for copy in copies:
            copy.start()
        for copy in copies:
            copy.wait()

    return pl.pallas_call(
        kernel,
        in_specs=[pl.BlockSpec(memory_space=pltpu.HBM)] * count,
        out_specs=[RESIDENT] * count,
        out_shape=[pltpu.VMEM(a.shape, a.dtype) for a in arrays],
        scratch_shapes=[pltpu.SemaphoreType.DMA((count,))],
        compiler_params=pltpu.CompilerParams(vmem_limit_bytes=1 << 20),
        cost_estimate=pl.CostEstimate(
            flops=0, bytes_accessed=sum(2 * a.size for a in arrays), transcendentals=0
        ),
        name="load",
    )(*in_hbm(arrays))


def slab(tile):
    return pl.ds(pl.multiple_of(pl.program_id(0) * tile, tile), tile)


def held(array):
    return pl.BlockSpec(
        array.shape, lambda i: (0,) * array.ndim, pipeline_mode=pl.Buffered(1)
    )


def columns(rows, tile):
    return pl.BlockSpec((rows, tile), lambda i: (0, i))


def forward_parts(pre_gate, pre_up):
    sigma = jax.nn.sigmoid(pre_gate)
    active = pre_gate * sigma
    slope = pre_up * sigma * (1.0 + pre_gate * (1.0 - sigma))
    return active, slope, active * pre_up


def stacked(refs):
    values = [ref[...] for ref in refs]
    return values[0] if len(values) == 1 else jnp.concatenate(values, axis=0)


def forward_rows(blocks, w_one, w_three):
    count, rows, (width, hidden) = len(blocks), sum(b.shape[0] for b in blocks), w_one.shape
    tile = tile_of(hidden, 512)

    def kernel(*refs):
        x_refs, (one, three, slope_ref, active_ref, hidden_ref) = refs[:count], refs[count:]
        x, here = stacked(x_refs), slab(tile)
        active, slope, product = forward_parts(
            jnp.dot(x, one[:, here], preferred_element_type=F32),
            jnp.dot(x, three[:, here], preferred_element_type=F32),
        )
        slope_ref[...] = slope.astype(BF16)
        active_ref[...] = active.astype(BF16)
        hidden_ref[...] = product.astype(BF16)

    return pl.pallas_call(
        kernel,
        grid=(hidden // tile,),
        in_specs=[held(b) for b in blocks] + [RESIDENT] * 2,
        out_specs=[columns(rows, tile)] * 3,
        out_shape=[pltpu.HBM((rows, hidden), BF16)] * 3,
        compiler_params=params(20),
        cost_estimate=pl.CostEstimate(
            flops=4 * rows * width * hidden,
            bytes_accessed=6 * rows * hidden,
            transcendentals=rows * hidden,
        ),
        name="forward_rows",
    )(*in_hbm(blocks), w_one, w_three)


def backward_rows(active_here, x_blocks, g, gates, w_one, w_three, w_two, parts):
    rows, (width, hidden) = g.shape[0], w_one.shape
    tile = tile_of(hidden, 512)
    count, height = len(x_blocks), sum(b.shape[0] for b in x_blocks)
    parts = parts or []

    def kernel(flag, *refs):
        x_refs, refs = refs[:count], refs[count:]
        g_ref, gate_ref, one, three, two, *refs = refs
        stored, refs = refs[: len(parts)], refs[len(parts) :]
        back_ref, part_ref, *made, total = refs
        step, here = pl.program_id(0), slab(tile)

        @pl.when(step == 0)
        def _():
            total[...] = jnp.zeros_like(total)
            part_ref[...] = jnp.zeros_like(part_ref)

        if made:
            x = stacked(x_refs)
            active, slope, product = forward_parts(
                jnp.dot(x, one[:, here], preferred_element_type=F32),
                jnp.dot(x, three[:, here], preferred_element_type=F32),
            )
            for ref, value in zip(made, (slope, active, product)):
                ref[...] = value.astype(BF16)

        @pl.when(flag[0] > 0)
        def _():
            slope_of, active_of, hidden_of = stored if parts else made
            back = jnp.dot(g_ref[...], two[...], preferred_element_type=F32)
            part_ref[...] += jnp.sum(hidden_of[...].astype(F32) * back, axis=1, keepdims=True)
            scaled = gate_ref[...] * back
            grad_gate = (scaled * slope_of[...].astype(F32)).astype(BF16)
            grad_up = (scaled * active_of[...].astype(F32)).astype(BF16)
            total[...] += lax.dot_general(
                grad_gate, one[:, here], BY_ROWS_T, preferred_element_type=F32
            ) + lax.dot_general(grad_up, three[:, here], BY_ROWS_T, preferred_element_type=F32)

        @pl.when(step == pl.num_programs(0) - 1)
        def _():
            back_ref[...] = total[...].astype(BF16)

    return pl.pallas_call(
        kernel,
        grid=(hidden // tile,),
        in_specs=[pl.BlockSpec(memory_space=pltpu.SMEM)]
        + [held(a) for a in (*x_blocks, g, gates)]
        + [RESIDENT] * 2
        + [columns(width, tile)]
        + [columns(rows, tile)] * len(parts),
        out_specs=[pl.BlockSpec((rows, width), lambda i: (0, 0)), pl.BlockSpec((rows, 1), lambda i: (0, 0))]
        + [columns(height, tile)] * (3 if count else 0),
        out_shape=[jax.ShapeDtypeStruct((rows, width), BF16), jax.ShapeDtypeStruct((rows, 1), F32)]
        + [pltpu.HBM((height, hidden), BF16)] * (3 if count else 0),
        scratch_shapes=[pltpu.VMEM((rows, width), F32)],
        compiler_params=params(20),
        cost_estimate=pl.CostEstimate(
            flops=(6 * rows + 4 * height) * width * hidden,
            bytes_accessed=2 * width * hidden,
            transcendentals=height * hidden,
        ),
        name="backward_rows",
    )(active_here.astype(jnp.int32).reshape(1), *in_hbm(x_blocks), g, gates, w_one, w_three, w_two, *in_hbm(parts))


def weight_grads(x_blocks, s_blocks, replica, cut, w_two, groups, before, scale):
    count, size, (width, hidden) = len(s_blocks), s_blocks[0].shape[0], w_two.shape
    rows = count * size
    tile = tile_of(hidden, 512 if rows <= 1024 else 256)
    sizes = [group[0].shape[0] for group in groups]
    aligned = cut % 128 == 0

    def kernel(*refs):
        x_cuts, refs = refs[1 : 1 + count], refs[1 + count :]
        s_cuts, refs = refs[:count], refs[count:]
        s_refs, two, refs = refs[:count], refs[count], refs[count + 1 :]
        given, refs = refs[: 3 * len(sizes)], refs[3 * len(sizes) :]
        sums, refs = refs[: len(before)], refs[len(before) :]
        out_one, out_three, out_two, x_turned, s_turned, grad_gate, grad_up, product = refs

        @pl.when(pl.program_id(0) == 0)
        def _():
            x_turned[...] = stacked(x_cuts).T
            s_turned[...] = stacked(s_cuts).T

        here_all = slab(tile)
        back = jnp.dot(stacked(s_refs), two[...], preferred_element_type=F32)
        start = 0
        for index, group_rows in enumerate(sizes):
            slope_ref, active_ref, hidden_ref = given[3 * index : 3 * index + 3]
            piece = back[start : start + group_rows, :]
            here = pl.ds(start, group_rows)
            grad_gate[here, :] = (piece * slope_ref[...].astype(F32)).astype(BF16)
            grad_up[here, :] = (piece * active_ref[...].astype(F32)).astype(BF16)
            product[here, :] = hidden_ref[...]
            start += group_rows

        for index, (out, left, right) in enumerate(
            ((out_one, x_turned, grad_gate), (out_three, x_turned, grad_up), (out_two, s_turned, product))
        ):
            value = jnp.dot(left[...], right[...], preferred_element_type=F32)
            if sums:
                value = sums[index][:, here_all] + value
            if scale is None:
                out[:, here_all] = value
            else:
                out[...] = (value * scale).astype(BF16)

    def by_tile(height):
        return pl.BlockSpec((height, tile), lambda i, at: (0, i))

    def kept_whole(shape, column=None):
        return pl.BlockSpec(shape, lambda i, at: (0, 0 if column is None else at[0]), pipeline_mode=pl.Buffered(1))

    if aligned:
        x_cuts, s_cuts = x_blocks, s_blocks
    else:
        x_cuts, s_cuts = (
            [lax.dynamic_slice_in_dim(b, replica * cut, cut, 1) for b in blocks] for blocks in (x_blocks, s_blocks)
        )
    place = replica if aligned else jnp.zeros_like(replica)
    return pl.pallas_call(
        kernel,
        grid_spec=pltpu.PrefetchScalarGridSpec(
            num_scalar_prefetch=1,
            grid=(hidden // tile,),
            in_specs=[kept_whole((size, cut), 0)] * (2 * count)
            + [kept_whole((size, width))] * count
            + [by_tile(width)]
            + [by_tile(group_rows) for group_rows in sizes for _ in range(3)]
            + [RESIDENT] * len(before),
            out_specs=[RESIDENT if scale is None else by_tile(cut)] * 3,
            scratch_shapes=[pltpu.VMEM((cut, rows), BF16)] * 2 + [pltpu.VMEM((rows, tile), BF16)] * 3,
        ),
        out_shape=[pltpu.VMEM((cut, hidden), F32) if scale is None else pltpu.HBM((cut, hidden), BF16)] * 3,
        compiler_params=params(24),
        cost_estimate=pl.CostEstimate(
            flops=2 * rows * width * hidden + 6 * rows * cut * hidden,
            bytes_accessed=2 * width * hidden + 6 * rows * hidden + 6 * cut * hidden,
            transcendentals=0,
        ),
        name="weight_grads",
    )(place.reshape(1).astype(jnp.int32), *in_hbm([*x_cuts, *s_cuts, *s_blocks, w_two]), *in_hbm([a for group in groups for a in group]), *before)


def ring_of(count):
    if count % 2:
        return list(range(count))
    return list(range(0, count, 2)) + list(range(count - 1, 0, -2))


def around(block, sections, count):
    walk = ring_of(count)

    def shift(step):
        return [
            (s * count + walk[i], s * count + walk[(i + step) % count])
            for s in range(sections)
            for i in range(count)
        ]

    axes = ("section", "dp")
    groups, ahead, behind = [[block]], block, block
    for _ in range(1, (count + 1) // 2):
        ahead = lax.ppermute(ahead, axes, shift(1))
        behind = lax.ppermute(behind, axes, shift(-1))
        groups.append([ahead, behind])
    if count % 2 == 0:
        half = block.shape[0] // 2
        front = lax.ppermute(ahead[:half], axes, shift(1))
        rear = lax.ppermute(behind[half:], axes, shift(-1))
        groups.append([jnp.concatenate([front, rear], axis=0)])
    return groups


def per_device(layer_inputs, out_grad, w_gate, w_up, w_down, slot_token, slot_gate):
    sections, replicas = lax.axis_size("section"), lax.axis_size("dp")
    last = lax.axis_index("section") == sections - 1
    half, replica = lax.axis_index("et"), lax.axis_index("dp")
    w_one, w_three, w_two = w_gate[0], w_up[0], w_down[0]
    x_mine, dy_mine = layer_inputs[0, 0], out_grad[0]
    slots, gates = slot_token[0, 0], slot_gate[0, 0][:, None]
    shard, width = x_mine.shape
    cut = width // replicas
    last_only = [(2 * (sections - 1) + e, 2 * (sections - 1) + 1 - e) for e in range(2)]
    first_only = [(e, 1 - e) for e in range(2)]

    def swapped(value, pairs):
        return lax.ppermute(value, ("section", "et"), pairs)

    def selector(of):
        return (slots[:, None] == of * shard + jnp.arange(shard, dtype=jnp.int32)[None, :]).astype(BF16)

    pick_mine, pick_theirs = selector(half), selector(1 - half)

    def picked(mine, theirs):
        return (
            jnp.dot(pick_mine, mine, preferred_element_type=F32)
            + jnp.dot(pick_theirs, theirs, preferred_element_type=F32)
        ).astype(BF16)

    def placed_back(pick, dy, back_mine, back_theirs):
        added = lax.dot_general(pick, back_mine, BY_ROWS, preferred_element_type=F32) + lax.dot_general(
            pick, back_theirs, BY_ROWS, preferred_element_type=F32
        )
        return (dy.astype(F32) + added).astype(BF16)

    dy_theirs = swapped(dy_mine, last_only)
    x_theirs = swapped(x_mine, last_only + first_only)
    w_one, w_three = load(w_one, w_three)
    x_rows = picked(x_mine, x_theirs)
    g_last = picked(dy_mine, dy_theirs)
    x_groups = around(x_rows, sections, replicas)

    def joined(groups):
        return [block for group in groups for block in group]

    back_last, part_last, *own = backward_rows(last, [x_rows], g_last, gates, w_one, w_three, w_two, None)
    other_last = swapped(back_last, last_only)
    ig_mine = placed_back(pick_mine, dy_mine, back_last, other_last)
    ig_theirs = placed_back(pick_theirs, dy_theirs, back_last, other_last)
    dy_first_mine = lax.ppermute(ig_mine, "section", [(1, 0)])
    dy_first_theirs = lax.ppermute(ig_theirs, "section", [(1, 0)])
    kept = [tuple(own), tuple(forward_rows(x_groups[1] + x_groups[2], w_one, w_three))]
    g_first = picked(dy_first_mine, dy_first_theirs)
    g_rows = jnp.where(last, g_last, g_first)
    s_rows = (gates * g_rows.astype(F32)).astype(BF16)
    s_groups = around(s_rows, sections, replicas)

    back_first, part_first = backward_rows(
        jnp.logical_not(last), [], g_first, gates, w_one, w_three, w_two, own
    )
    other_first = swapped(back_first, first_only)
    part = jnp.where(last, part_last, part_first)[:, 0]
    gate_grad = part + lax.ppermute(part, "et", first_only)
    ig_first = placed_back(pick_mine, dy_first_mine, back_first, other_first)
    in_grad = jnp.where(last, ig_mine, ig_first)
    rest = joined(x_groups[3:])
    late = []
    for start in range(0, len(rest), 4):
        late.append(tuple(forward_rows(rest[start : start + 4], w_one, w_three)))

    sums = weight_grads(joined(x_groups[:3]), joined(s_groups[:3]), replica, cut, w_two, kept, [], None)
    far = joined(s_groups[3:])
    for index, group in enumerate(late):
        scale = 1.0 / replicas if index == len(late) - 1 else None
        here = slice(4 * index, 4 * index + 4)
        sums = weight_grads(rest[here], far[here], replica, cut, w_two, [group], sums, scale)
    return (in_grad[None, None], *[grad[None] for grad in sums], gate_grad[None, None])


def solution(mesh):
    placed = (
        P("section", None, ("dp", "et"), None),
        P(None, ("dp", "et"), None),
        P("section", None, "et"),
        P("section", None, "et"),
        P("section", None, "et"),
        P("section", None, "dp"),
        P("section", None, "dp"),
    )

    return jax.shard_map(
        per_device,
        mesh=mesh,
        in_specs=placed,
        out_specs=(
            P("section", None, ("dp", "et"), None),
            P("section", "dp", "et"),
            P("section", "dp", "et"),
            P("section", "dp", "et"),
            P("section", None, "dp"),
        ),
        check_vma=False,
    )
```
